32 devices in a mesh: gx: 4 (over z), gy: 8 (over y, x, core).
Axes of the slice: x: 2, y: 2, z: 4, core: 2. Of those that a mesh axis runs over, the one named last changes fastest.
Arguments:
- right_side: float32 [32, 128, 128], P('gx', 'gy'), may hold values from -8 to 8
- diagonal: float32 [32, 128, 128], P('gx', 'gy'), may hold values from 0.25 to 2
- solid_mask: int32 [32, 128, 128], P('gx', 'gy'), may hold values 0 or 1
- geneo_vectors: bfloat16 [32, 32, 128, 128], P(None, 'gx', 'gy'), may hold values from -0.046875 to 0.046875
- vector_counts: int32 [4, 8], P('gx', 'gy'), may hold values from 8 to 32, as said below
- owner_slots: int32 [32], replicated, may hold values from 0 to 31, each once
- coarse_inverse: float32 [1024, 64], P('gy'), may hold values from -1 to 8, as said below
Outputs:
- solution: float32 [32, 128, 128], P('gx', 'gy')
- residual: float32 [32, 128, 128], P('gx', 'gy')
The draws below stay inside these ranges and needn't reach their ends.
Inputs may be any that keep to these rules, and one draw needn't show every extreme that they name: `vector_counts`: every count lies between 8 and 32; both ends occur in every draw. Subdomain s belongs to coarse block owner_slots[s] // 2. `coarse_inverse`: each block is symmetric positive definite; rows and columns beyond a subdomain's count are unused.
All inputs are finite; a program needn't handle non-finite values. No bound on the sum of `solid_mask` on one device may be relied on, other than what follows from the above.
Results may differ from the reference program's by a relative error of at most 0.0003.
Values sent between devices are 32-bit elements; how exact they have to be, the bound alone decides.
No kernel may reach another device: no remote copies, remote signals or barrier semaphores. Data moves between devices by JAX's collectives and lax.ppermute only.
A program may use at most 64 MiB of HBM per device.

```python
import jax
import jax.numpy as jnp
from jax import lax

CX = 8
CY = 16
CZ = 128
KMAX = 32
OWNERS = 16
DEG = 3
ITERS = 2
SUBX = 4
SUBY = 8
NSUB = 32
BLK = 64
NX = 32
NY = 128


def draw_vector_counts(key, part):
    total = SUBX * SUBY
    values = jax.random.randint(key, (total,), KMAX // 4, KMAX + 1)
    where = jax.random.randint(jax.random.fold_in(key, 1), (), 0, total)
    values = values.at[where].set(KMAX)
    values = values.at[(where + 1) % total].set(KMAX // 4)
    return values.reshape(SUBX, SUBY).astype(jnp.int32)


def draw_coarse_inverse(key, part):
    spread = jax.random.uniform(key, (OWNERS, BLK, BLK), jnp.float32, -1.0, 1.0) / jnp.sqrt(jnp.float32(BLK))
    sym = 0.5 * (spread + jnp.swapaxes(spread, 1, 2))
    diag_vals = jax.random.uniform(jax.random.fold_in(key, 2), (OWNERS, BLK), jnp.float32, 2.0, 4.0)
    index = jnp.arange(BLK)
    eye_mat = (index[:, None] == index[None, :]).astype(jnp.float32)
    whole = sym * (1.0 - eye_mat)[None] + eye_mat[None] * diag_vals[:, :, None]
    return whole.reshape(OWNERS * BLK, BLK)


def touch_ends(result, rng, low, largest):
    longest = result.shape.index(max(result.shape))
    spots = []
    for shift in (0, 1):
        where = [jax.random.randint(jax.random.fold_in(rng, axis), (), 0, length) for axis, length in enumerate(result.shape)]
        where[longest] = (where[longest] + shift) % result.shape[longest]
        spots.append(tuple(where))
    return result.at[spots[0]].set(low).at[spots[1]].set(largest)


def levels(rng, dims, pieces, least, largest):
    def one(dim, parts):
        steps = jax.random.uniform(jax.random.fold_in(jax.random.fold_in(rng, 6), dim), (parts,), jnp.float32, least / len(pieces), largest / len(pieces))
        return jnp.repeat(jnp.exp(steps), dims[dim] // parts).reshape((-1,) + (1,) * (len(dims) - dim - 1))

    loudness = one(*pieces[0])
    for cut in pieces[1:]:
        loudness = loudness * one(*cut)
    return loudness


def centred(key, dims, scale, bound, split=(), held_as=jnp.bfloat16):
    result = jax.random.normal(key, dims, jnp.float32) * scale
    if len(split) > 0:
        result = levels(key, dims, split, -0.22, 0.18) * result
    return jnp.clip(result, min=-bound, max=bound).astype(held_as)


def setup_inputs(seed: int = 0) -> dict:
    keys = jax.random.split(jax.random.key(seed), 8)
    right_side = centred(keys[0], (NX, NY, CZ), 1.0, 8.0, ((0, 4), (1, 8)), jnp.float32)
    diagonal = jnp.clip(0.25 + 1.75 * jax.random.uniform(keys[1], (NX, NY, CZ), jnp.float32) ** levels(keys[1], (NX, NY, CZ), ((0, 4), (1, 8)), -0.2, 0.2), 0.25, 2.0)
    solid_mask = touch_ends((jax.random.randint(keys[2], (NX, NY, CZ), 0, 8) < 1).astype(jnp.int32), jax.random.fold_in(keys[2], 1), 0, 1)
    geneo_vectors = centred(keys[3], (KMAX, NX, NY, CZ), (CX * CY * CZ) ** -0.5, 0.046875, ((1, 4), (2, 8)))
    vector_counts = draw_vector_counts(jax.random.fold_in(keys[7], 71), 0)
    owner_slots = jax.random.permutation(keys[5], NSUB).astype(jnp.int32)
    coarse_inverse = draw_coarse_inverse(jax.random.fold_in(keys[7], 71), 0)
    return {"right_side": right_side, "diagonal": diagonal, "solid_mask": solid_mask, "geneo_vectors": geneo_vectors, "vector_counts": vector_counts, "owner_slots": owner_slots, "coarse_inverse": coarse_inverse}


CHEB_LO = 0.3
CHEB_HI = 2.0
HIGH = lax.Precision.HIGHEST


def operate(field, diagonal, fluid):
    masked = fluid * field
    padded = jnp.pad(masked, 1)
    beside = padded[2:, 1:-1, 1:-1] + padded[:-2, 1:-1, 1:-1]
    beside = beside + padded[1:-1, 2:, 1:-1] + padded[1:-1, :-2, 1:-1]
    beside = beside + padded[1:-1, 1:-1, 2:] + padded[1:-1, 1:-1, :-2]
    return fluid * ((6.0 + diagonal) * field - beside) + (1.0 - fluid) * field


def smoother(res, diagonal, fluid, jacobi):
    centre = (CHEB_HI + CHEB_LO) / 2.0
    half_width = (CHEB_HI - CHEB_LO) / 2.0
    sigma_val = centre / half_width
    rho_old = 1.0 / sigma_val
    update = jacobi * res / centre
    smooth = update
    remainder = res
    for repeat in range(DEG - 1):
        remainder = remainder - operate(update, diagonal, fluid)
        rho_new = 1.0 / (2.0 * sigma_val - rho_old)
        update = rho_new * rho_old * update + (2.0 * rho_new / half_width) * jacobi * remainder
        smooth = smooth + update
        rho_old = rho_new
    return smooth


def reference(right_side, diagonal, solid_mask, geneo_vectors, vector_counts, owner_slots, coarse_inverse):
    fluid = 1.0 - solid_mask.astype(jnp.float32)
    jacobi = 1.0 / (fluid * (6.0 + diagonal) + 1.0 - fluid)
    live = (jnp.arange(KMAX, dtype=jnp.int32)[None, None, :] < vector_counts[:, :, None]).astype(jnp.float32)
    vectors = jnp.moveaxis(geneo_vectors.reshape(KMAX, SUBX, CX, SUBY, CY, CZ), 1, 0)
    inverse = coarse_inverse.reshape(OWNERS, BLK, BLK)

    def project_row(items):
        zrow, rrow = items
        return jnp.einsum("kaybz,aybz->yk", zrow.astype(jnp.float32), rrow, precision=HIGH)

    def prolong_row(items):
        zrow, crow = items
        return jnp.einsum("kaybz,yk->aybz", zrow.astype(jnp.float32), crow, precision=HIGH)

    def precondition(res):
        smooth = smoother(res, diagonal, fluid, jacobi)
        rows = res.reshape(SUBX, CX, SUBY, CY, CZ)
        projected = lax.map(project_row, (vectors, rows)) * live
        ordered = jnp.zeros((NSUB, KMAX), jnp.float32).at[owner_slots].set(projected.reshape(NSUB, KMAX))
        coarse = jnp.einsum("obc,oc->ob", inverse, ordered.reshape(OWNERS, BLK), precision=HIGH)
        coeffs = coarse.reshape(NSUB, KMAX)[owner_slots].reshape(SUBX, SUBY, KMAX) * live
        fine = lax.map(prolong_row, (vectors, coeffs))
        return smooth + fine.reshape(NX, NY, CZ)

    solution = jnp.zeros_like(right_side)
    residual = right_side
    precond = precondition(residual)
    direction = precond
    norm_now = jnp.sum(residual * precond)
    for repeat in range(ITERS):
        image = operate(direction, diagonal, fluid)
        step_len = norm_now / jnp.sum(direction * image)
        solution = solution + step_len * direction
        residual = residual - step_len * image
        if repeat + 1 < ITERS:
            precond = precondition(residual)
            norm_next = jnp.sum(residual * precond)
            direction = precond + (norm_next / norm_now) * direction
            norm_now = norm_next
    return solution, residual
```

```python
import functools

import jax
import jax.numpy as jnp
from jax import lax
from jax.experimental import pallas as pl
from jax.experimental.pallas import tpu as pltpu
from jax.sharding import PartitionSpec as P

DEG = 3
CHEB_LO = 0.3
CHEB_HI = 2.0
H = 4
HR = 2
LANES = 128
VMEM = pl.BlockSpec(memory_space=pltpu.VMEM)
SMEM = pl.BlockSpec(memory_space=pltpu.SMEM)


def call(body, out, *args, scratch=(), smem=0):
    shapes = [jax.ShapeDtypeStruct(s, jnp.float32) for s in out]
    return pl.pallas_call(
        body,
        out_shape=shapes,
        in_specs=[SMEM] * smem + [VMEM] * (len(args) - smem),
        out_specs=[VMEM] * len(out),
        scratch_shapes=list(scratch),
    )(*args)


def beside(masked):
    rows, lanes = masked[0].shape
    lane = lax.broadcasted_iota(jnp.int32, (rows, lanes), 1)
    first, last = lane == 0, lane == lanes - 1
    out = []
    for i in range(1, len(masked) - 1):
        mid = masked[i]
        total = masked[i + 1] + masked[i - 1]
        total = total + pltpu.roll(mid, 1, 0) + pltpu.roll(mid, rows - 1, 0)
        total = total + jnp.where(first, 0.0, pltpu.roll(mid, 1, 1))
        total = total + jnp.where(last, 0.0, pltpu.roll(mid, lanes - 1, 1))
        out.append(total)
    return out


def operate(field, centre, fluid):
    near = beside([f * v for f, v in zip(fluid, field)])
    n = len(field)
    return [centre[i] * field[i] - fluid[i] * near[i - 1] for i in range(1, n - 1)]


def inner(rows, k):
    return rows[k:len(rows) - k] if k else rows


def smoother(res, centre, fluid, jacobi):
    theta = (CHEB_HI + CHEB_LO) / 2.0
    delta = (CHEB_HI - CHEB_LO) / 2.0
    sigma = theta / delta
    rho = 1.0 / sigma
    update = [j * r * (1.0 / theta) for j, r in zip(jacobi, res)]
    smooth = update
    rest = res
    for step in range(DEG - 1):
        image = operate(update, inner(centre, step), inner(fluid, step))
        rest = [a - b for a, b in zip(inner(rest, 1), image)]
        rho_new = 1.0 / (2.0 * sigma - rho)
        near_j = inner(jacobi, step + 1)
        update = [
            rho_new * rho * u + (2.0 * rho_new / delta) * (j * r)
            for u, j, r in zip(inner(update, 1), near_j, rest)
        ]
        smooth = [a + b for a, b in zip(inner(smooth, 1), update)]
        rho = rho_new
    return smooth


def total(rows):
    acc = rows[0]
    for r in rows[1:]:
        acc = acc + r
    return jnp.sum(jnp.sum(acc, axis=0, keepdims=True), axis=1, keepdims=True)


def lane_group(width):
    return lax.broadcasted_iota(jnp.int32, (1, LANES), 1) // width


def project(vec_ref, rows, count):
    kcount, nx = vec_ref.shape[:2]
    sums = []
    for k in range(kcount):
        acc = None
        for i in range(nx):
            term = vec_ref[k, i].astype(jnp.float32) * rows[i]
            acc = term if acc is None else acc + term
        sums.append(jnp.sum(acc, axis=0, keepdims=True))
    col = jnp.sum(jnp.concatenate(sums, axis=0), axis=1, keepdims=True)
    lane = lax.broadcasted_iota(jnp.int32, (kcount, LANES), 1)
    row = lax.broadcasted_iota(jnp.int32, (kcount, LANES), 0)
    picked = jnp.where((lane % kcount == row) & (row < count), col, 0.0)
    return jnp.sum(picked, axis=0, keepdims=True)


def prolong(vec_ref, coeffs):
    kcount, nx, ny, nz = vec_ref.shape
    rows = [None] * nx
    for k in range(kcount):
        scale = jnp.broadcast_to(coeffs[k], (ny, nz))
        for i in range(nx):
            term = vec_ref[k, i].astype(jnp.float32) * scale
            rows[i] = term if rows[i] is None else rows[i] + term
    return rows


class Plan:
    def __init__(self, mesh, kcount, row_count, block):
        self.gx, self.gy = mesh.shape["gx"], mesh.shape["gy"]
        self.devices = self.gx * self.gy
        self.kcount, self.row_count, self.block = kcount, row_count, block
        self.held = row_count // kcount
        self.members = block // kcount
        self.piece = kcount // self.gx
        self.lines = self.piece * block // LANES
        assert self.piece * self.gx == kcount and self.lines * LANES == self.piece * block
        assert self.gx % 2 == 0 and self.gy % 2 == 0


def invert(slots_ref, inv_ref):
    def body(t, carry):
        inv_ref[slots_ref[t]] = t
        return carry

    lax.fori_loop(0, slots_ref.shape[0], body, 0, unroll=slots_ref.shape[0] <= 64)


def coarse(plan, slots_ref, inv_ref, recv_p_ref, recv_w_ref, count):
    me = lax.axis_index("gx") * plan.gy + lax.axis_index("gy")
    slot = slots_ref[me]
    first = slot // plan.members * plan.members
    holder = slot * plan.kcount // plan.row_count
    group = lane_group(plan.kcount)
    groups = LANES // plan.kcount
    wide = max(1, plan.block // LANES)
    rhs = []
    for q in range(wide):
        row = None
        for g in range(groups):
            m = (q * LANES + g * plan.kcount) % plan.block // plan.kcount
            part = recv_p_ref[inv_ref[first + m], :, 0:LANES]
            row = part if row is None else jnp.where(group == g, part, row)
        rhs.append(row)
    coeffs = []
    split = max(1, LANES // plan.block)
    part_of = lane_group(LANES // split)
    for c in range(plan.gx):
        src = c * plan.gy + holder
        lines = [
            recv_w_ref[src, :, LANES * (1 + a):LANES * (2 + a)] * rhs[a % wide]
            for a in range(plan.lines)
        ]
        if wide > 1:
            lines = [sum(lines[a + 1:a + wide], lines[a]) for a in range(0, plan.lines, wide)]
        for line in lines:
            for s in range(split):
                piece = jnp.where(part_of == s, line, 0.0) if split > 1 else line
                coeffs.append(jnp.sum(piece, axis=1, keepdims=True))
    return [jnp.where(k < count, v, 0.0) for k, v in enumerate(coeffs)]


def pick(parity, low, high):
    even = parity == 0
    return jnp.where(even, high, low), jnp.where(even, low, high)


def prep_kernel(rhs_ref, diag_ref, solid_ref, centre_ref, fluid_ref, a_ref, b_ref):
    nx, ny, _ = rhs_ref.shape
    parity = lax.axis_index("gy") % 2
    fluid = 1.0 - solid_ref[...].astype(jnp.float32)
    centre = fluid * (6.0 + diag_ref[...]) + 1.0 - fluid
    fluid_ref[...] = fluid
    centre_ref[...] = centre
    for f, value in enumerate((centre, fluid, rhs_ref[...])):
        a, b = pick(parity, value[:, :H], value[:, ny - H:])
        a_ref[f * nx:(f + 1) * nx] = a
        b_ref[f * nx:(f + 1) * nx] = b


def first_kernel(plan, slots_ref, count_ref, rhs_ref, vec_ref, inv_rows_ref, msg_ref, inv_ref):
    nx = rhs_ref.shape[0]
    invert(slots_ref, inv_ref)
    proj = project(vec_ref, [rhs_ref[i] for i in range(nx)], count_ref[0, 0])
    msg_ref[:, :, 0:LANES] = jnp.broadcast_to(proj[None], (plan.devices, 1, LANES))
    gx, gy = lax.axis_index("gx"), lax.axis_index("gy")
    for k in range(plan.held):
        dest = inv_ref[gy * plan.held + k]
        rows = inv_rows_ref[k * plan.gx + gx]
        for a in range(plan.lines):
            msg_ref[dest, :, LANES * (1 + a):LANES * (2 + a)] = rows[a:a + 1]


def widen(own, a, b, parity):
    even = parity == 0
    return jnp.concatenate([jnp.where(even, b, a), own, jnp.where(even, a, b)], axis=1)


def static_mid_kernel(size, rhs_ref, centre_ref, fluid_ref, ya_ref, yb_ref,
                      c_ref, f_ref, r_ref, a_ref, b_ref):
    nx, ny, _ = rhs_ref.shape
    gy = lax.axis_index("gy")
    fields = []
    for f, own in enumerate((centre_ref, fluid_ref, rhs_ref)):
        part = slice(f * nx, (f + 1) * nx)
        fields.append(widen(own[...], ya_ref[part], yb_ref[part], gy % 2))
    centre, fluid, rhs = fields
    col = lax.broadcasted_iota(jnp.int32, centre.shape, 1)
    out = ((col < H) & (gy == 0)) | ((col >= ny + H) & (gy == size - 1))
    c_ref[...] = jnp.where(out, 1.0, centre)
    f_ref[...] = jnp.where(out, 0.0, fluid)
    r_ref[...] = rhs
    low = lax.axis_index("gx") % 2
    high = 1 - low
    at = 0
    for ref, width in ((c_ref, H), (f_ref, H), (r_ref, HR)):
        a_ref[at:at + width] = ref[pl.ds(high * (nx - width), width)]
        b_ref[at:at + width] = ref[pl.ds(low * (nx - width), width)]
        at += width


def start_kernel(size, c_ref, f_ref, r_ref, xa_ref, xb_ref,
                 centre_ref, fluid_ref, jacobi_ref, u_ref, rhs_ref):
    nx = c_ref.shape[0]
    ny = u_ref.shape[1]
    gx = lax.axis_index("gx")
    odd = gx % 2
    at = 0
    for own, ref, width in ((c_ref, centre_ref, H), (f_ref, fluid_ref, H), (r_ref, rhs_ref, HR)):
        ref[width:width + nx] = own[...]
        ref[pl.ds((1 - odd) * (nx + width), width)] = xa_ref[at:at + width]
        ref[pl.ds(odd * (nx + width), width)] = xb_ref[at:at + width]
        at += width

    @pl.when(gx == 0)
    def _():
        centre_ref[0:H] = jnp.ones_like(centre_ref[0:H])
        fluid_ref[0:H] = jnp.zeros_like(fluid_ref[0:H])

    @pl.when(gx == size - 1)
    def _():
        centre_ref[nx + H:] = jnp.ones_like(centre_ref[nx + H:])
        fluid_ref[nx + H:] = jnp.zeros_like(fluid_ref[nx + H:])

    jacobi_ref[...] = 1.0 / centre_ref[...]
    cut = H - HR
    span = range(cut, nx + 2 * H - cut)
    rows = smoother(
        [rhs_ref[i] for i in range(nx + 2 * HR)],
        [centre_ref[i] for i in span],
        [fluid_ref[i] for i in span],
        [jacobi_ref[i] for i in span],
    )
    for i in range(nx):
        u_ref[i] = rows[i][H:H + ny]


def direction_kernel(plan, slots_ref, count_ref, recv_ref, u_ref, rhs_ref, vec_ref,
                     d_ref, a_ref, b_ref, norm_ref, inv_ref):
    nx, ny, _ = u_ref.shape
    invert(slots_ref, inv_ref)
    coeffs = coarse(plan, slots_ref, inv_ref, recv_ref, recv_ref, count_ref[0, 0])
    rows = [u_ref[i] + f for i, f in enumerate(prolong(vec_ref, coeffs))]
    parity = lax.axis_index("gy") % 2
    for i in range(nx):
        d_ref[i] = rows[i]
        a_ref[i], b_ref[i] = pick(parity, rows[i][:H], rows[i][ny - H:])
    norm_ref[...] = jnp.broadcast_to(total([rhs_ref[i] * rows[i] for i in range(nx)]), (1, LANES))


def direction_mid_kernel(d_ref, ya_ref, yb_ref, dy_ref, a_ref, b_ref):
    nx = d_ref.shape[0]
    dy_ref[...] = widen(d_ref[...], ya_ref[...], yb_ref[...], lax.axis_index("gy") % 2)
    low = lax.axis_index("gx") % 2
    a_ref[...] = dy_ref[pl.ds((1 - low) * (nx - H), H)]
    b_ref[...] = dy_ref[pl.ds(low * (nx - H), H)]


def image_kernel(count_ref, dy_ref, xa_ref, xb_ref, d_ref, centre_ref, fluid_ref, jacobi_ref,
                 vec_ref, norm_ref, w_ref, u_ref, au_ref, msg_ref, wide_ref):
    nx, ny, _ = d_ref.shape
    odd = lax.axis_index("gx") % 2
    wide_ref[H:H + nx] = dy_ref[...]
    wide_ref[pl.ds((1 - odd) * (nx + H), H)] = xa_ref[...]
    wide_ref[pl.ds(odd * (nx + H), H)] = xb_ref[...]
    span = range(nx + 2 * H)
    centre = [centre_ref[i] for i in span]
    fluid = [fluid_ref[i] for i in span]
    jacobi = [jacobi_ref[i] for i in span]
    image = operate([wide_ref[i] for i in span], centre, fluid)
    smooth = smoother(image, inner(centre, 1), inner(fluid, 1), inner(jacobi, 1))
    image_u = operate(smooth, inner(centre, 3), inner(fluid, 3))
    w = [row[H:H + ny] for row in inner(image, H - 1)]
    for i in range(nx):
        w_ref[i] = w[i]
        u_ref[i] = smooth[i + 1][H:H + ny]
        au_ref[i] = image_u[i][H:H + ny]
    proj = project(vec_ref, w, count_ref[0, 0])
    curve = total([d_ref[i] * w[i] for i in range(nx)])
    sums = jnp.where(lane_group(32) == 0, norm_ref[...], curve)
    msg_ref[:, :, 0:LANES] = jnp.broadcast_to(proj[None], (msg_ref.shape[0], 1, LANES))
    msg_ref[:, :, LANES:] = jnp.broadcast_to(sums[None], (msg_ref.shape[0], 1, LANES))


def fine_kernel(plan, slots_ref, count_ref, recv_ref, recv_w_ref, vec_ref, fluid_ref,
                f_ref, ya_ref, yb_ref, xa_ref, xb_ref, inv_ref):
    nx, ny, _ = f_ref.shape
    invert(slots_ref, inv_ref)
    coeffs = coarse(plan, slots_ref, inv_ref, recv_ref, recv_w_ref, count_ref[0, 0])
    rows = prolong(vec_ref, coeffs)
    for i in range(nx):
        f_ref[i] = rows[i]
    masked = [r * fluid_ref[i] for i, r in enumerate(rows)]
    parity = lax.axis_index("gy") % 2
    for i in range(nx):
        ya_ref[i], yb_ref[i] = pick(parity, masked[i][:1], masked[i][ny - 1:])
    a, b = pick(lax.axis_index("gx") % 2, masked[0], masked[nx - 1])
    xa_ref[0] = a
    xb_ref[0] = b


def finish_kernel(plan, f_ref, ya_ref, yb_ref, xa_ref, xb_ref, u_ref, au_ref, w_ref, rhs_ref,
                  centre_ref, fluid_ref, z_ref, az_ref, msg_ref):
    nx, ny, nz = f_ref.shape
    gx, gy = lax.axis_index("gx"), lax.axis_index("gy")
    even_x, even_y = gx % 2 == 0, gy % 2 == 0
    lowest = jnp.where(even_x, xb_ref[0], xa_ref[0])
    highest = jnp.where(even_x, xa_ref[0], xb_ref[0])
    lowest = jnp.where(gx == 0, 0.0, lowest)
    highest = jnp.where(gx == plan.gx - 1, 0.0, highest)
    fine = [f_ref[i] for i in range(nx)]
    fluid = [fluid_ref[i] for i in range(nx)]
    masked = [lowest] + [a * b for a, b in zip(fine, fluid)] + [highest]
    lane = lax.broadcasted_iota(jnp.int32, (ny, nz), 1)
    row = lax.broadcasted_iota(jnp.int32, (ny, nz), 0)
    one, two, three = [], [], []
    for i in range(nx):
        mid = masked[i + 1]
        ya, yb = ya_ref[i], yb_ref[i]
        left = jnp.where(gy == 0, 0.0, jnp.where(even_y, yb, ya))
        right = jnp.where(gy == plan.gy - 1, 0.0, jnp.where(even_y, ya, yb))
        near = masked[i] + masked[i + 2]
        near = near + jnp.where(row == 0, left, pltpu.roll(mid, 1, 0))
        near = near + jnp.where(row == ny - 1, right, pltpu.roll(mid, ny - 1, 0))
        near = near + jnp.where(lane == 0, 0.0, pltpu.roll(mid, 1, 1))
        near = near + jnp.where(lane == nz - 1, 0.0, pltpu.roll(mid, nz - 1, 1))
        z = u_ref[i] + fine[i]
        az = au_ref[i] + (centre_ref[i] * fine[i] - fluid[i] * near)
        z_ref[i] = z
        az_ref[i] = az
        one.append(rhs_ref[i] * z)
        two.append(w_ref[i] * z)
        three.append(z * az)
    group = lane_group(32)
    sums = jnp.where(group == 0, total(one), jnp.where(group == 1, total(two), total(three)))
    msg_ref[...] = jnp.broadcast_to(sums[None], msg_ref.shape)


def last_kernel(recv2_ref, recv3_ref, rhs_ref, d_ref, w_ref, z_ref, az_ref, x_ref, r_ref):
    nx, ny, nz = d_ref.shape
    first = jnp.sum(recv2_ref[:, :, LANES:], axis=0)
    second = jnp.sum(recv3_ref[...], axis=0)
    norm, curve = first[:, 0:1], first[:, 32:33]
    rz, wz, zaz = second[:, 0:1], second[:, 32:33], second[:, 64:65]
    step = norm / curve
    norm_new = norm - step * (rz + curve) + step * step * wz
    ratio = norm_new / norm
    along = curve - step * wz
    bend = along - step * wz + step * step * zaz
    bend = bend + 2.0 * ratio * along + ratio * ratio * curve
    step_new = norm_new / bend
    shape = (ny, nz)
    on_d = jnp.broadcast_to(step + step_new * (1.0 + ratio), shape)
    on_z = jnp.broadcast_to(step_new * step, shape)
    for i in range(nx):
        x_ref[i] = on_d * d_ref[i] - on_z * z_ref[i]
        r_ref[i] = rhs_ref[i] - (on_d * w_ref[i] - on_z * az_ref[i])


def swap(a, b, axis):
    n = lax.axis_size(axis)
    even = [(i, i ^ 1) for i in range(n)]
    odd = [(i, (i + 1) % n if i % 2 else (i - 1) % n) for i in range(n)]
    return lax.ppermute(a, axis, even), lax.ppermute(b, axis, odd)


def exchange(msg):
    return lax.all_to_all(msg, ("gx", "gy"), 0, 0, tiled=True)


def on_device(mesh, rhs, diagonal, solid, vectors, counts, slots, inverse):
    nx, ny, nz = rhs.shape
    plan = Plan(mesh, vectors.shape[0], inverse.shape[0], inverse.shape[1])
    cells = (nx, ny, nz)
    side = (nx, ny + 2 * H, nz)
    wide = (nx + 2 * H, ny + 2 * H, nz)
    n = plan.devices
    inv_scratch = [pltpu.SMEM((n,), jnp.int32)]
    with_plan = lambda body: functools.partial(body, plan)

    inv_rows = inverse.reshape(plan.held * plan.gx, plan.lines, LANES)
    face = (3 * nx, H, nz)
    centre, fluid, a, b = call(prep_kernel, [cells, cells, face, face], rhs, diagonal, solid)
    ya, yb = swap(a, b, "gy")
    (msg1,) = call(with_plan(first_kernel), [(n, 1, LANES * (1 + plan.lines))],
                   slots, counts, rhs, vectors, inv_rows, scratch=inv_scratch, smem=2)
    recv1 = exchange(msg1)
    face = (2 * H + HR, ny + 2 * H, nz)
    c_y, f_y, r_y, a, b = call(functools.partial(static_mid_kernel, plan.gy),
                               [side, side, side, face, face], rhs, centre, fluid, ya, yb)
    xa, xb = swap(a, b, "gx")
    c_w, f_w, j_w, smooth, _ = call(functools.partial(start_kernel, plan.gx),
                                    [wide, wide, wide, cells, (nx + 2 * HR, ny + 2 * H, nz)],
                                    c_y, f_y, r_y, xa, xb)
    face = (nx, H, nz)
    direction, a, b, norm = call(with_plan(direction_kernel), [cells, face, face, (1, LANES)],
                                 slots, counts, recv1, smooth, rhs, vectors,
                                 scratch=inv_scratch, smem=2)
    ya, yb = swap(a, b, "gy")
    face = (H, ny + 2 * H, nz)
    d_y, a, b = call(direction_mid_kernel, [side, face, face], direction, ya, yb)
    xa, xb = swap(a, b, "gx")
    image, smooth, image_u, msg2 = call(
        image_kernel, [cells, cells, cells, (n, 1, 2 * LANES)],
        counts, d_y, xa, xb, direction, c_w, f_w, j_w, vectors, norm,
        scratch=[pltpu.VMEM(wide, jnp.float32)], smem=1)
    recv2 = exchange(msg2)
    fine, ya, yb, xa, xb = call(
        with_plan(fine_kernel), [cells, (nx, 1, nz), (nx, 1, nz), (1, ny, nz), (1, ny, nz)],
        slots, counts, recv2, recv1, vectors, fluid, scratch=inv_scratch, smem=2)
    ya, yb = swap(ya, yb, "gy")
    xa, xb = swap(xa, xb, "gx")
    z, image_z, msg3 = call(with_plan(finish_kernel), [cells, cells, (n, 1, LANES)],
                            fine, ya, yb, xa, xb, smooth, image_u, image, rhs, centre, fluid)
    recv3 = exchange(msg3)
    return tuple(call(last_kernel, [cells, cells],
                      recv2, recv3, rhs, direction, image, z, image_z))


def solution(mesh):
    in_specs = (
        P("gx", "gy", None),
        P("gx", "gy", None),
        P("gx", "gy", None),
        P(None, "gx", "gy", None),
        P("gx", "gy"),
        P(),
        P("gy", None),
    )
    out_specs = (P("gx", "gy", None), P("gx", "gy", None))
    return jax.shard_map(
        functools.partial(on_device, mesh), mesh=mesh, in_specs=in_specs, out_specs=out_specs,
        check_vma=False,
    )
```

```python
import functools

import jax
import jax.numpy as jnp
from jax import lax
from jax.experimental import pallas as pl
from jax.experimental.pallas import tpu as pltpu
from jax.sharding import PartitionSpec as P

DEG = 3
CHEB_LO = 0.3
CHEB_HI = 2.0
H = 4
HR = 2
LANES = 128
VMEM_GRANT = 16 * 2**20
VMEM = pl.BlockSpec(memory_space=pltpu.VMEM)
SMEM = pl.BlockSpec(memory_space=pltpu.SMEM)


def call(body, out, *args, scratch=(), smem=0):
    shapes = [jax.ShapeDtypeStruct(s, jnp.float32) for s in out]
    return pl.pallas_call(
        body,
        out_shape=shapes,
        in_specs=[SMEM] * smem + [VMEM] * (len(args) - smem),
        out_specs=[VMEM] * len(out),
        scratch_shapes=list(scratch),
        compiler_params=pltpu.CompilerParams(vmem_limit_bytes=VMEM_GRANT),
    )(*args)


def beside(masked):
    rows, lanes = masked[0].shape
    lane = lax.broadcasted_iota(jnp.int32, (rows, lanes), 1)
    first, last = lane == 0, lane == lanes - 1
    out = []
    for i in range(1, len(masked) - 1):
        mid = masked[i]
        total = masked[i + 1] + masked[i - 1]
        total = total + pltpu.roll(mid, 1, 0) + pltpu.roll(mid, rows - 1, 0)
        total = total + jnp.where(first, 0.0, pltpu.roll(mid, 1, 1))
        total = total + jnp.where(last, 0.0, pltpu.roll(mid, lanes - 1, 1))
        out.append(total)
    return out


def operate(field, centre, fluid):
    near = beside([f * v for f, v in zip(fluid, field)])
    n = len(field)
    return [centre[i] * field[i] - fluid[i] * near[i - 1] for i in range(1, n - 1)]


def inner(rows, k):
    return rows[k:len(rows) - k] if k else rows


def smoother(res, centre, fluid, jacobi):
    theta = (CHEB_HI + CHEB_LO) / 2.0
    delta = (CHEB_HI - CHEB_LO) / 2.0
    sigma = theta / delta
    rho = 1.0 / sigma
    update = [j * r * (1.0 / theta) for j, r in zip(jacobi, res)]
    smooth = update
    rest = res
    for step in range(DEG - 1):
        image = operate(update, inner(centre, step), inner(fluid, step))
        rest = [a - b for a, b in zip(inner(rest, 1), image)]
        rho_new = 1.0 / (2.0 * sigma - rho)
        near_j = inner(jacobi, step + 1)
        update = [
            rho_new * rho * u + (2.0 * rho_new / delta) * (j * r)
            for u, j, r in zip(inner(update, 1), near_j, rest)
        ]
        smooth = [a + b for a, b in zip(inner(smooth, 1), update)]
        rho = rho_new
    return smooth


def total(rows):
    acc = rows[0]
    for r in rows[1:]:
        acc = acc + r
    return jnp.sum(jnp.sum(acc, axis=0, keepdims=True), axis=1, keepdims=True)


def lane_group(width):
    return lax.broadcasted_iota(jnp.int32, (1, LANES), 1) // width


def project(vec_ref, rows, count):
    kcount, nx = vec_ref.shape[:2]
    sums = []
    for k in range(kcount):
        acc = None
        for i in range(nx):
            term = vec_ref[k, i].astype(jnp.float32) * rows[i]
            acc = term if acc is None else acc + term
        sums.append(jnp.sum(acc, axis=0, keepdims=True))
    col = jnp.sum(jnp.concatenate(sums, axis=0), axis=1, keepdims=True)
    lane = lax.broadcasted_iota(jnp.int32, (kcount, LANES), 1)
    row = lax.broadcasted_iota(jnp.int32, (kcount, LANES), 0)
    picked = jnp.where((lane % kcount == row) & (row < count), col, 0.0)
    return jnp.sum(picked, axis=0, keepdims=True)


def prolong(vec_ref, coeffs):
    kcount, nx, ny, nz = vec_ref.shape
    rows = [None] * nx
    for k in range(kcount):
        scale = jnp.broadcast_to(coeffs[k], (ny, nz))
        for i in range(nx):
            term = vec_ref[k, i].astype(jnp.float32) * scale
            rows[i] = term if rows[i] is None else rows[i] + term
    return rows


class Plan:
    def __init__(self, mesh, kcount, row_count, block):
        self.gx, self.gy = mesh.shape["gx"], mesh.shape["gy"]
        self.devices = self.gx * self.gy
        self.kcount, self.row_count, self.block = kcount, row_count, block
        self.held = row_count // kcount
        self.members = block // kcount
        self.piece = kcount // self.gx
        self.lines = self.piece * block // LANES
        assert self.piece * self.gx == kcount and self.lines * LANES == self.piece * block
        assert self.gx % 2 == 0 and self.gy % 2 == 0


def invert(slots_ref, inv_ref):
    def body(t, carry):
        inv_ref[slots_ref[t]] = t
        return carry

    lax.fori_loop(0, slots_ref.shape[0], body, 0, unroll=slots_ref.shape[0] <= 64)


def coarse(plan, slots_ref, inv_ref, recv_p_ref, recv_w_ref, count):
    me = lax.axis_index("gx") * plan.gy + lax.axis_index("gy")
    slot = slots_ref[me]
    first = slot // plan.members * plan.members
    holder = slot * plan.kcount // plan.row_count
    group = lane_group(plan.kcount)
    groups = LANES // plan.kcount
    wide = max(1, plan.block // LANES)
    rhs = []
    for q in range(wide):
        row = None
        for g in range(groups):
            m = (q * LANES + g * plan.kcount) % plan.block // plan.kcount
            part = recv_p_ref[inv_ref[first + m], :, 0:LANES]
            row = part if row is None else jnp.where(group == g, part, row)
        rhs.append(row)
    coeffs = []
    split = max(1, LANES // plan.block)
    part_of = lane_group(LANES // split)
    for c in range(plan.gx):
        src = c * plan.gy + holder
        lines = [
            recv_w_ref[src, :, LANES * (1 + a):LANES * (2 + a)] * rhs[a % wide]
            for a in range(plan.lines)
        ]
        if wide > 1:
            lines = [sum(lines[a + 1:a + wide], lines[a]) for a in range(0, plan.lines, wide)]
        for line in lines:
            for s in range(split):
                piece = jnp.where(part_of == s, line, 0.0) if split > 1 else line
                coeffs.append(jnp.sum(piece, axis=1, keepdims=True))
    return [jnp.where(k < count, v, 0.0) for k, v in enumerate(coeffs)]


def pick(parity, low, high):
    even = parity == 0
    return jnp.where(even, high, low), jnp.where(even, low, high)


def prep_kernel(rhs_ref, diag_ref, solid_ref, centre_ref, fluid_ref, a_ref, b_ref):
    nx, ny, _ = rhs_ref.shape
    parity = lax.axis_index("gy") % 2
    fluid = 1.0 - solid_ref[...].astype(jnp.float32)
    centre = fluid * (6.0 + diag_ref[...]) + 1.0 - fluid
    fluid_ref[...] = fluid
    centre_ref[...] = centre
    for f, value in enumerate((centre, fluid, rhs_ref[...])):
        a, b = pick(parity, value[:, :H], value[:, ny - H:])
        a_ref[f * nx:(f + 1) * nx] = a
        b_ref[f * nx:(f + 1) * nx] = b


def first_kernel(plan, slots_ref, count_ref, rhs_ref, vec_ref, inv_rows_ref, msg_ref, inv_ref):
    nx = rhs_ref.shape[0]
    invert(slots_ref, inv_ref)
    proj = project(vec_ref, [rhs_ref[i] for i in range(nx)], count_ref[0, 0])
    msg_ref[:, :, 0:LANES] = jnp.broadcast_to(proj[None], (plan.devices, 1, LANES))
    gx, gy = lax.axis_index("gx"), lax.axis_index("gy")
    for k in range(plan.held):
        dest = inv_ref[gy * plan.held + k]
        rows = inv_rows_ref[k * plan.gx + gx]
        for a in range(plan.lines):
            msg_ref[dest, :, LANES * (1 + a):LANES * (2 + a)] = rows[a:a + 1]


def widen(own, a, b, parity):
    even = parity == 0
    return jnp.concatenate([jnp.where(even, b, a), own, jnp.where(even, a, b)], axis=1)


def static_mid_kernel(size, rhs_ref, centre_ref, fluid_ref, ya_ref, yb_ref,
                      c_ref, f_ref, r_ref, a_ref, b_ref):
    nx, ny, _ = rhs_ref.shape
    gy = lax.axis_index("gy")
    fields = []
    for f, own in enumerate((centre_ref, fluid_ref, rhs_ref)):
        part = slice(f * nx, (f + 1) * nx)
        fields.append(widen(own[...], ya_ref[part], yb_ref[part], gy % 2))
    centre, fluid, rhs = fields
    col = lax.broadcasted_iota(jnp.int32, centre.shape, 1)
    out = ((col < H) & (gy == 0)) | ((col >= ny + H) & (gy == size - 1))
    c_ref[...] = jnp.where(out, 1.0, centre)
    f_ref[...] = jnp.where(out, 0.0, fluid)
    r_ref[...] = rhs
    low = lax.axis_index("gx") % 2
    high = 1 - low
    at = 0
    for ref, width in ((c_ref, H), (f_ref, H), (r_ref, HR)):
        a_ref[at:at + width] = ref[pl.ds(high * (nx - width), width)]
        b_ref[at:at + width] = ref[pl.ds(low * (nx - width), width)]
        at += width


def start_kernel(size, c_ref, f_ref, r_ref, xa_ref, xb_ref,
                 centre_ref, fluid_ref, jacobi_ref, u_ref, rhs_ref):
    nx = c_ref.shape[0]
    ny = u_ref.shape[1]
    gx = lax.axis_index("gx")
    odd = gx % 2
    at = 0
    for own, ref, width in ((c_ref, centre_ref, H), (f_ref, fluid_ref, H), (r_ref, rhs_ref, HR)):
        ref[width:width + nx] = own[...]
        ref[pl.ds((1 - odd) * (nx + width), width)] = xa_ref[at:at + width]
        ref[pl.ds(odd * (nx + width), width)] = xb_ref[at:at + width]
        at += width

    @pl.when(gx == 0)
    def _():
        centre_ref[0:H] = jnp.ones_like(centre_ref[0:H])
        fluid_ref[0:H] = jnp.zeros_like(fluid_ref[0:H])

    @pl.when(gx == size - 1)
    def _():
        centre_ref[nx + H:] = jnp.ones_like(centre_ref[nx + H:])
        fluid_ref[nx + H:] = jnp.zeros_like(fluid_ref[nx + H:])

    jacobi_ref[...] = 1.0 / centre_ref[...]
    cut = H - HR
    span = range(cut, nx + 2 * H - cut)
    rows = smoother(
        [rhs_ref[i] for i in range(nx + 2 * HR)],
        [centre_ref[i] for i in span],
        [fluid_ref[i] for i in span],
        [jacobi_ref[i] for i in span],
    )
    for i in range(nx):
        u_ref[i] = rows[i][H:H + ny]


def direction_kernel(plan, slots_ref, count_ref, recv_ref, u_ref, rhs_ref, vec_ref,
                     d_ref, a_ref, b_ref, norm_ref, inv_ref):
    nx, ny, _ = u_ref.shape
    invert(slots_ref, inv_ref)
    coeffs = coarse(plan, slots_ref, inv_ref, recv_ref, recv_ref, count_ref[0, 0])
    rows = [u_ref[i] + f for i, f in enumerate(prolong(vec_ref, coeffs))]
    parity = lax.axis_index("gy") % 2
    for i in range(nx):
        d_ref[i] = rows[i]
        a_ref[i], b_ref[i] = pick(parity, rows[i][:H], rows[i][ny - H:])
    norm_ref[...] = jnp.broadcast_to(total([rhs_ref[i] * rows[i] for i in range(nx)]), (1, LANES))


def direction_mid_kernel(d_ref, ya_ref, yb_ref, dy_ref, a_ref, b_ref):
    nx = d_ref.shape[0]
    dy_ref[...] = widen(d_ref[...], ya_ref[...], yb_ref[...], lax.axis_index("gy") % 2)
    low = lax.axis_index("gx") % 2
    a_ref[...] = dy_ref[pl.ds((1 - low) * (nx - H), H)]
    b_ref[...] = dy_ref[pl.ds(low * (nx - H), H)]


def image_kernel(count_ref, dy_ref, xa_ref, xb_ref, d_ref, centre_ref, fluid_ref, jacobi_ref,
                 vec_ref, norm_ref, w_ref, u_ref, au_ref, msg_ref, wide_ref):
    nx, ny, _ = d_ref.shape
    odd = lax.axis_index("gx") % 2
    wide_ref[H:H + nx] = dy_ref[...]
    wide_ref[pl.ds((1 - odd) * (nx + H), H)] = xa_ref[...]
    wide_ref[pl.ds(odd * (nx + H), H)] = xb_ref[...]
    span = range(nx + 2 * H)
    centre = [centre_ref[i] for i in span]
    fluid = [fluid_ref[i] for i in span]
    jacobi = [jacobi_ref[i] for i in span]
    image = operate([wide_ref[i] for i in span], centre, fluid)
    smooth = smoother(image, inner(centre, 1), inner(fluid, 1), inner(jacobi, 1))
    image_u = operate(smooth, inner(centre, 3), inner(fluid, 3))
    w = [row[H:H + ny] for row in inner(image, H - 1)]
    for i in range(nx):
        w_ref[i] = w[i]
        u_ref[i] = smooth[i + 1][H:H + ny]
        au_ref[i] = image_u[i][H:H + ny]
    proj = project(vec_ref, w, count_ref[0, 0])
    curve = total([d_ref[i] * w[i] for i in range(nx)])
    sums = jnp.where(lane_group(32) == 0, norm_ref[...], curve)
    msg_ref[:, :, 0:LANES] = jnp.broadcast_to(proj[None], (msg_ref.shape[0], 1, LANES))
    msg_ref[:, :, LANES:] = jnp.broadcast_to(sums[None], (msg_ref.shape[0], 1, LANES))


def fine_kernel(plan, slots_ref, count_ref, recv_ref, recv_w_ref, vec_ref, fluid_ref,
                f_ref, ya_ref, yb_ref, xa_ref, xb_ref, inv_ref):
    nx, ny, _ = f_ref.shape
    invert(slots_ref, inv_ref)
    coeffs = coarse(plan, slots_ref, inv_ref, recv_ref, recv_w_ref, count_ref[0, 0])
    rows = prolong(vec_ref, coeffs)
    for i in range(nx):
        f_ref[i] = rows[i]
    masked = [r * fluid_ref[i] for i, r in enumerate(rows)]
    parity = lax.axis_index("gy") % 2
    for i in range(nx):
        ya_ref[i], yb_ref[i] = pick(parity, masked[i][:1], masked[i][ny - 1:])
    a, b = pick(lax.axis_index("gx") % 2, masked[0], masked[nx - 1])
    xa_ref[0] = a
    xb_ref[0] = b


def finish_kernel(plan, f_ref, ya_ref, yb_ref, xa_ref, xb_ref, u_ref, au_ref, w_ref, rhs_ref,
                  centre_ref, fluid_ref, z_ref, az_ref, msg_ref):
    nx, ny, nz = f_ref.shape
    gx, gy = lax.axis_index("gx"), lax.axis_index("gy")
    even_x, even_y = gx % 2 == 0, gy % 2 == 0
    lowest = jnp.where(even_x, xb_ref[0], xa_ref[0])
    highest = jnp.where(even_x, xa_ref[0], xb_ref[0])
    lowest = jnp.where(gx == 0, 0.0, lowest)
    highest = jnp.where(gx == plan.gx - 1, 0.0, highest)
    fine = [f_ref[i] for i in range(nx)]
    fluid = [fluid_ref[i] for i in range(nx)]
    masked = [lowest] + [a * b for a, b in zip(fine, fluid)] + [highest]
    lane = lax.broadcasted_iota(jnp.int32, (ny, nz), 1)
    row = lax.broadcasted_iota(jnp.int32, (ny, nz), 0)
    one, two, three = [], [], []
    for i in range(nx):
        mid = masked[i + 1]
        ya, yb = ya_ref[i], yb_ref[i]
        left = jnp.where(gy == 0, 0.0, jnp.where(even_y, yb, ya))
        right = jnp.where(gy == plan.gy - 1, 0.0, jnp.where(even_y, ya, yb))
        near = masked[i] + masked[i + 2]
        near = near + jnp.where(row == 0, left, pltpu.roll(mid, 1, 0))
        near = near + jnp.where(row == ny - 1, right, pltpu.roll(mid, ny - 1, 0))
        near = near + jnp.where(lane == 0, 0.0, pltpu.roll(mid, 1, 1))
        near = near + jnp.where(lane == nz - 1, 0.0, pltpu.roll(mid, nz - 1, 1))
        z = u_ref[i] + fine[i]
        az = au_ref[i] + (centre_ref[i] * fine[i] - fluid[i] * near)
        z_ref[i] = z
        az_ref[i] = az
        one.append(rhs_ref[i] * z)
        two.append(w_ref[i] * z)
        three.append(z * az)
    group = lane_group(32)
    sums = jnp.where(group == 0, total(one), jnp.where(group == 1, total(two), total(three)))
    msg_ref[...] = jnp.broadcast_to(sums[None], msg_ref.shape)


def last_kernel(recv2_ref, recv3_ref, rhs_ref, d_ref, w_ref, z_ref, az_ref, x_ref, r_ref):
    nx, ny, nz = d_ref.shape
    first = jnp.sum(recv2_ref[:, :, LANES:], axis=0)
    second = jnp.sum(recv3_ref[...], axis=0)
    norm, curve = first[:, 0:1], first[:, 32:33]
    rz, wz, zaz = second[:, 0:1], second[:, 32:33], second[:, 64:65]
    step = norm / curve
    norm_new = norm - step * (rz + curve) + step * step * wz
    ratio = norm_new / norm
    along = curve - step * wz
    bend = along - step * wz + step * step * zaz
    bend = bend + 2.0 * ratio * along + ratio * ratio * curve
    step_new = norm_new / bend
    shape = (ny, nz)
    on_d = jnp.broadcast_to(step + step_new * (1.0 + ratio), shape)
    on_z = jnp.broadcast_to(step_new * step, shape)
    for i in range(nx):
        x_ref[i] = on_d * d_ref[i] - on_z * z_ref[i]
        r_ref[i] = rhs_ref[i] - (on_d * w_ref[i] - on_z * az_ref[i])


def swap(a, b, axis):
    n = lax.axis_size(axis)
    even = [(i, i ^ 1) for i in range(n)]
    odd = [(i, (i + 1) % n if i % 2 else (i - 1) % n) for i in range(n)]
    return lax.ppermute(a, axis, even), lax.ppermute(b, axis, odd)


def exchange(msg):
    return lax.all_to_all(msg, ("gx", "gy"), 0, 0, tiled=True)


def on_device(mesh, rhs, diagonal, solid, vectors, counts, slots, inverse):
    nx, ny, nz = rhs.shape
    plan = Plan(mesh, vectors.shape[0], inverse.shape[0], inverse.shape[1])
    cells = (nx, ny, nz)
    side = (nx, ny + 2 * H, nz)
    wide = (nx + 2 * H, ny + 2 * H, nz)
    n = plan.devices
    inv_scratch = [pltpu.SMEM((n,), jnp.int32)]
    with_plan = lambda body: functools.partial(body, plan)

    inv_rows = inverse.reshape(plan.held * plan.gx, plan.lines, LANES)
    face = (3 * nx, H, nz)
    centre, fluid, a, b = call(prep_kernel, [cells, cells, face, face], rhs, diagonal, solid)
    ya, yb = swap(a, b, "gy")
    (msg1,) = call(with_plan(first_kernel), [(n, 1, LANES * (1 + plan.lines))],
                   slots, counts, rhs, vectors, inv_rows, scratch=inv_scratch, smem=2)
    recv1 = exchange(msg1)
    face = (2 * H + HR, ny + 2 * H, nz)
    c_y, f_y, r_y, a, b = call(functools.partial(static_mid_kernel, plan.gy),
                               [side, side, side, face, face], rhs, centre, fluid, ya, yb)
    xa, xb = swap(a, b, "gx")
    c_w, f_w, j_w, smooth, _ = call(functools.partial(start_kernel, plan.gx),
                                    [wide, wide, wide, cells, (nx + 2 * HR, ny + 2 * H, nz)],
                                    c_y, f_y, r_y, xa, xb)
    face = (nx, H, nz)
    direction, a, b, norm = call(with_plan(direction_kernel), [cells, face, face, (1, LANES)],
                                 slots, counts, recv1, smooth, rhs, vectors,
                                 scratch=inv_scratch, smem=2)
    ya, yb = swap(a, b, "gy")
    face = (H, ny + 2 * H, nz)
    d_y, a, b = call(direction_mid_kernel, [side, face, face], direction, ya, yb)
    xa, xb = swap(a, b, "gx")
    image, smooth, image_u, msg2 = call(
        image_kernel, [cells, cells, cells, (n, 1, 2 * LANES)],
        counts, d_y, xa, xb, direction, c_w, f_w, j_w, vectors, norm,
        scratch=[pltpu.VMEM(wide, jnp.float32)], smem=1)
    recv2 = exchange(msg2)
    fine, ya, yb, xa, xb = call(
        with_plan(fine_kernel), [cells, (nx, 1, nz), (nx, 1, nz), (1, ny, nz), (1, ny, nz)],
        slots, counts, recv2, recv1, vectors, fluid, scratch=inv_scratch, smem=2)
    ya, yb = swap(ya, yb, "gy")
    xa, xb = swap(xa, xb, "gx")
    z, image_z, msg3 = call(with_plan(finish_kernel), [cells, cells, (n, 1, LANES)],
                            fine, ya, yb, xa, xb, smooth, image_u, image, rhs, centre, fluid)
    recv3 = exchange(msg3)
    return tuple(call(last_kernel, [cells, cells],
                      recv2, recv3, rhs, direction, image, z, image_z))


def solution(mesh):
    in_specs = (
        P("gx", "gy", None),
        P("gx", "gy", None),
        P("gx", "gy", None),
        P(None, "gx", "gy", None),
        P("gx", "gy"),
        P(),
        P("gy", None),
    )
    out_specs = (P("gx", "gy", None), P("gx", "gy", None))
    return jax.shard_map(
        functools.partial(on_device, mesh), mesh=mesh, in_specs=in_specs, out_specs=out_specs,
        check_vma=False,
    )
```
